512 devices in a mesh: space: 64 (over x, y, core), snap: 8 (over z).
Axes of the slice: x: 4, y: 8, z: 8, core: 2. Of those that a mesh axis runs over, the one named last changes fastest.
Arguments:
- velocity: bfloat16 [128, 3, 256, 32, 128], P('snap', None, 'space'), may hold values from -8 to 8
- metric: float32 [3, 256, 32, 128], P(None, 'space'), may hold values from 0.5 to 2
- volume: float32 [256, 32, 128], P('space'), may hold values from 0.3 to 9
- coeffs: bfloat16 [128, 128], replicated, may hold values from -0.5 to 0.5
Outputs:
- gram: float32 [128, 128], P('snap')
- modes: bfloat16 [128, 3, 256, 32, 128], P('snap', None, 'space')
The draws below stay inside these ranges and needn't reach their ends.
All inputs are finite; a program needn't handle non-finite values.
Results may differ from the reference program's by a relative error of at most 0.0004.
The reference program's roundings to bfloat16 on the way (of `vorticity` and `weighted`) count: a program that leaves them out, or rounds other values in their place, can miss the bound.
Values may be sent and summed in bfloat16 or wider, within the bound.
A program may use at most 64 MiB of HBM per device.

```python
import math
import jax
import jax.numpy as jnp
from jax import lax

SNAPS = 128
NY = 32
NZ = 128
NX = 256


def draw_volume(key, part):
    place = jnp.arange(NX, dtype=jnp.float32)
    rising = 1.0 + 2.0 * place / (NX - 1)
    base = jnp.exp(jax.random.uniform(key, (NX, NY, NZ), jnp.float32, jnp.log(0.5), jnp.log(2.0)))
    return base * rising[:, None, None]


def draw_velocity(key, part):
    shared = 12
    cells = 3 * NX * NY * NZ
    key_fields = jax.random.fold_in(key, 101)
    key_amps = jax.random.fold_in(key, 202)
    key_noise = jax.random.fold_in(key, 303)
    order = jnp.arange(shared, dtype=jnp.float32)
    weights = 0.6 * jnp.power(0.85, order)
    amps = jax.random.normal(key_amps, (SNAPS, shared), jnp.float32) * weights[None, :]
    fields = jax.random.normal(key_fields, (shared, cells), jnp.float32)
    noise = jax.random.normal(key_noise, (SNAPS, cells), jnp.float32)
    mixed = jnp.dot(amps, fields) + 0.4 * noise
    mixed = jnp.clip(mixed, -8.0, 8.0)
    return mixed.reshape(SNAPS, 3, NX, NY, NZ).astype(jnp.bfloat16)


def block_scale(own_key, dims, pieces, low, top_value):
    def one(position, parts):
        draws = jax.random.uniform(jax.random.fold_in(jax.random.fold_in(own_key, 6), position), (parts,), jnp.float32, low / len(pieces), top_value / len(pieces))
        return jnp.repeat(jnp.exp(draws), dims[position] // parts).reshape((-1,) + (1,) * (len(dims) - position - 1))

    gain = one(*pieces[0])
    for cut in pieces[1:]:
        gain = gain * one(*cut)
    return gain


def scatter_about(stream_key, shape, deviation, reach, held_as=jnp.bfloat16):
    values = deviation * jax.random.normal(stream_key, shape, jnp.float32)
    return jnp.clip(values, min=-reach, max=reach).astype(held_as)


def setup_inputs(seed: int = 0) -> dict:
    arg_keys = jax.random.split(jax.random.key(seed), 5)
    velocity = draw_velocity(jax.random.fold_in(arg_keys[4], 71), 0)
    metric = jnp.clip(jnp.exp(math.log(2.0) - 1.3862944 * jax.random.uniform(arg_keys[1], (3, NX, NY, NZ), jnp.float32) ** block_scale(arg_keys[1], (3, NX, NY, NZ), ((1, 64),), -0.2, 0.2)), 0.5, 2.0)
    volume = draw_volume(jax.random.fold_in(arg_keys[4], 71), 0)
    coeffs = scatter_about(arg_keys[3], (SNAPS, SNAPS), SNAPS ** -0.5, 0.5)
    return {"velocity": velocity, "metric": metric, "volume": volume, "coeffs": coeffs}


def deriv(padded, dim):
    count = padded.shape[dim] - 4

    def cut(offset):
        return lax.slice_in_dim(padded, offset, offset + count, axis=dim)
    return (8.0 * (cut(3) - cut(1)) - (cut(4) - cut(0))) / 12.0

def curl(padded_x, metric):
    inner = padded_x[:, :, 2:-2]
    padded_y = jnp.pad(inner, ((0, 0), (0, 0), (0, 0), (2, 2), (0, 0)))
    padded_z = jnp.concatenate([inner[..., -2:], inner, inner[..., :2]], axis=4)
    along_x = deriv(padded_x, 2) * metric[0]
    along_y = deriv(padded_y, 3) * metric[1]
    along_z = deriv(padded_z, 4) * metric[2]
    omega_x = along_y[:, 2] - along_z[:, 1]
    omega_y = along_z[:, 0] - along_x[:, 2]
    omega_z = along_x[:, 1] - along_y[:, 0]
    return jnp.stack([omega_x, omega_y, omega_z], axis=1).astype(jnp.bfloat16)

def reference(velocity, metric, volume, coeffs):

    def single(snapshot):
        padded = jnp.concatenate([snapshot[:, -2:], snapshot, snapshot[:, :2]], axis=1)[None]
        return curl(padded.astype(jnp.float32), metric)[0]
    vorticity = lax.map(single, velocity)
    snaps = velocity.shape[0]
    weighted = (vorticity.astype(jnp.float32) * volume).astype(jnp.bfloat16).reshape(snaps, -1)
    flat = vorticity.reshape(snaps, -1)
    scale = 1.0 / (3.0 * volume.shape[0] * volume.shape[1] * volume.shape[2])
    gram = lax.dot_general(weighted, flat, (((1,), (1,)), ((), ())), preferred_element_type=jnp.float32) * scale
    coeff_f = coeffs.astype(jnp.float32)
    energy = lax.optimization_barrier(jnp.sum(coeff_f * jnp.dot(gram, coeff_f, precision=lax.Precision.HIGHEST), axis=0))
    raw = lax.dot_general(coeffs, flat, (((0,), (0,)), ((), ())), preferred_element_type=jnp.float32)
    modes = (raw / jnp.sqrt(energy + 1e-06)[:, None]).astype(jnp.bfloat16).reshape(vorticity.shape)
    return (gram, modes)
```

```python
import functools

import jax
import jax.numpy as jnp
from jax import lax
from jax.experimental import pallas as pl
from jax.experimental.pallas import tpu as pltpu
from jax.sharding import PartitionSpec as P

EPS = 1e-06
MESH = pl.DeviceIdType.MESH
F32 = jnp.float32
BF16 = jnp.bfloat16
HALF = 16
GROUP = 4


def remote(src, dst, send, recv, where):
    return pltpu.make_async_remote_copy(
        src_ref=src, dst_ref=dst, send_sem=send, recv_sem=recv,
        device_id=where, device_id_type=MESH,
    )


def kernel(
    ny, nz, nxc, cells,
    vel, metric, volume, coeffs,
    out, gram_out,
    ext, vort, got, raw, mbuf, coeff_t, acc, col, e_send, e_got, g_own, g_got0, g_send, g_got,
    local_sem, halo_ss, halo_rs, a_ss, a_rs, m_ss, m_rs, e_ss, e_rs, g_ss, g_rs,
):
    s = lax.axis_index("space")
    z = lax.axis_index("snap")
    nspace = ny * nxc
    core, iy, ix = lax.rem(s, 2), lax.rem(s // 2, ny), s // (2 * ny)
    q = ix * 2 + core
    left, right = lax.rem(s + nspace - 1, nspace), lax.rem(s + 1, nspace)

    def z_peer(k):
        return lax.rem(z + k, nz)

    def y_peer(k):
        return (ix * ny + lax.rem(iy + k, ny)) * 2 + core

    def q_peer(k):
        other = lax.rem(q + k, nxc)
        return ((other // 2) * ny + iy) * 2 + lax.rem(other, 2)

    barrier = pltpu.get_barrier_semaphore()
    for k in range(1, nz):
        pl.semaphore_signal(barrier, inc=1, device_id={"snap": z_peer(k)}, device_id_type=MESH)
    for k in range(1, ny):
        pl.semaphore_signal(barrier, inc=1, device_id={"space": y_peer(k)}, device_id_type=MESH)
    for k in range(1, nxc):
        pl.semaphore_signal(barrier, inc=1, device_id={"space": q_peer(k)}, device_id_type=MESH)
    for side in (left, right):
        pl.semaphore_signal(barrier, inc=1, device_id={"space": side}, device_id_type=MESH)

    loads = [
        pltpu.make_async_copy(vel.at[c], ext.at[c, 2:6, 2:34], local_sem.at[c]) for c in range(3)
    ]
    for c in (2, 1, 0):
        loads[c].start()
    blank = jnp.zeros((4, 2, 16, 128), BF16)
    for c in (0, 2):
        ext[c, 2:6, 0:2] = blank
        ext[c, 2:6, 34:36] = blank
    coeff_t[...] = coeffs[...].astype(F32).T.astype(BF16)
    acc[...] = jnp.zeros_like(acc)
    loads[2].wait()
    loads[1].wait()

    def tile(c, layer, row):
        return ext[c, layer, row].astype(F32)

    def stencil(a, b, c, d):
        return 8.0 * (c - b) - (d - a)

    def along_x(c, layer, row):
        return stencil(*[tile(c, layer + o, row + 2) for o in (0, 1, 3, 4)])

    def along_y(c, layer, row):
        return stencil(*[tile(c, layer + 2, row + o) for o in (0, 1, 3, 4)])

    def along_z(c, layer, row):
        f = tile(c, layer + 2, row + 2)
        return stencil(*[pltpu.roll(f, o % 128, 1) for o in (2, 1, -1, -2)])

    def factor(d, layer, row):
        return metric[d, layer, pl.ds(row, 1), :] * (1.0 / 12.0)

    def curl(c, layer, row):
        if c == 0:
            a = along_y(2, layer, row) * factor(1, layer, row)
            b = along_z(1, layer, row) * factor(2, layer, row)
        elif c == 1:
            a = along_z(0, layer, row) * factor(2, layer, row)
            b = along_x(2, layer, row) * factor(0, layer, row)
        else:
            a = along_x(1, layer, row) * factor(0, layer, row)
            b = along_y(0, layer, row) * factor(1, layer, row)
        return (a - b).astype(BF16)

    def place(part):
        return part // 2, lax.rem(part, 2) * HALF

    def part_curl(c, part):
        layer, low = place(part)

        def step(i, carry):
            for j in range(GROUP):
                row = low + i * GROUP + j
                vort[c, layer, row] = curl(c, layer, row)
            return carry

        lax.fori_loop(0, HALF // GROUP, step, 0)

    def part_send(c, k):
        peer = z_peer(k)
        layer, low = place(peer)
        return remote(
            vort.at[c, layer, pl.ds(low, HALF)], got.at[c, :, z],
            a_ss.at[c, k], a_rs.at[c, k], {"snap": peer},
        )

    def own_part(c):
        layer, low = place(z)
        return pltpu.make_async_copy(
            vort.at[c, layer, pl.ds(low, HALF)], got.at[c, :, z], a_ss.at[c, 0]
        )

    order = [k for pair in zip(range(nz // 2, 0, -1), range(nz // 2 + 1, nz + 1)) for k in pair]
    order = [k for k in order if k < nz]

    def exchange(c, after=None):
        if after is not None:
            for k in order:
                part_curl(c, z_peer(k))
            after()
            for k in order:
                part_send(c, k).start()
        else:
            for k in order:
                part_curl(c, z_peer(k))
                part_send(c, k).start()
        part_curl(c, z)
        own_part(c).start()

    def halo(c, side):
        n = 2 * (2 - c) + side
        if side == 0:
            return remote(
                ext.at[c, 2:4, 2:34], ext.at[c, 6:8, 2:34], halo_ss.at[n], halo_rs.at[n], {"space": left}
            )
        return remote(
            ext.at[c, 4:6, 2:34], ext.at[c, 0:2, 2:34], halo_ss.at[n], halo_rs.at[n], {"space": right}
        )

    def enter():
        pl.semaphore_wait(barrier, (nz - 1) + (ny - 1) + (nxc - 1) + 2)
        for c in (2, 1):
            for side in (0, 1):
                halo(c, side).start()

    exchange(0, enter)
    loads[0].wait()
    for c, needs in ((1, 2), (2, 1)):
        for side in (0, 1):
            halo(needs, side).wait_recv()
        exchange(c)

    my_layer, my_low = place(z)

    def wide(c, i):
        rows = [got[c, i * GROUP + j].reshape(128, 128) for j in range(GROUP)]
        return jnp.concatenate(rows, axis=1)

    def arrived(c):
        for k in order:
            part_send(c, k).wait_recv()
        own_part(c).wait()

    def gram_of(c):
        def step(i, carry):
            v = wide(c, i)
            cells_volume = jnp.concatenate(
                [volume[my_layer, pl.ds(my_low + i * GROUP + j, 1), :] for j in range(GROUP)], axis=1
            )
            w = (v.astype(F32) * cells_volume).astype(BF16)
            acc[...] += lax.dot_general(w, v, (((1,), (1,)), ((), ())), preferred_element_type=F32)
            return carry

        lax.fori_loop(0, HALF // GROUP, step, 0)

    def raw_of(c):
        def step(i, carry):
            r = jnp.dot(coeff_t[...], wide(c, i), preferred_element_type=F32)
            for j in range(GROUP):
                raw[c, i * GROUP + j] = r[:, 128 * j : 128 * (j + 1)]
            return carry

        lax.fori_loop(0, HALF // GROUP, step, 0)

    for c in range(3):
        arrived(c)
        gram_of(c)
        if c < 2:
            raw_of(c)

    g_own[...] = acc[...] * (1.0 / cells)
    coeff_f = coeffs[...].astype(F32)
    product = jnp.dot(g_own[...], coeff_f, precision=lax.Precision.HIGHEST, preferred_element_type=F32)
    partial_e = jnp.sum((product * coeff_f).reshape(16, 8, 128), axis=0)
    stages = (
        (nz, z, lambda k: {"snap": z_peer(k)}),
        (ny, iy, lambda k: {"space": y_peer(k)}),
        (nxc, q, lambda k: {"space": q_peer(k)}),
    )

    def e_copy(stage, k):
        _, mine, where = stages[stage]
        return remote(
            e_send.at[stage], e_got.at[stage, mine], e_ss.at[stage, k], e_rs.at[stage, k], where(k)
        )

    def g_copy0(k):
        peer = z_peer(k)
        return remote(
            g_own.at[pl.ds(pl.multiple_of(peer * 16, 16), 16)], g_got0.at[z],
            g_ss.at[0, k], g_rs.at[0, k], {"snap": peer},
        )

    def g_copy(stage, k):
        _, mine, where = stages[stage]
        return remote(
            g_send.at[stage], g_got.at[stage, mine], g_ss.at[stage, k], g_rs.at[stage, k], where(k)
        )

    for stage, (count, mine, _) in enumerate(stages):
        e_send[stage] = partial_e
        e_got[stage, mine] = partial_e
        for k in range(1, count):
            e_copy(stage, k).start()
        if stage == 0:
            for k in range(1, nz):
                g_copy0(k).start()
            raw_of(2)
        for k in range(1, count):
            e_copy(stage, k).wait_recv()
        partial_e = e_got[stage, 0]
        for i in range(1, count):
            partial_e = partial_e + e_got[stage, i]
    energy = jnp.sum(partial_e, axis=0, keepdims=True)
    inverse = 1.0 / jnp.sqrt(energy + EPS)
    at_row = lax.broadcasted_iota(jnp.int32, (128, 128), 0)
    at_lane = lax.broadcasted_iota(jnp.int32, (128, 128), 1)
    diagonal = jnp.where(at_row == at_lane, jnp.broadcast_to(inverse, (128, 128)), 0.0)
    col[...] = jnp.broadcast_to(jnp.sum(diagonal, axis=1, keepdims=True), (128, 128))

    def modes_for(group):
        first = pl.multiple_of(group * 16, 16)
        scale = col[pl.ds(first, 16), :]

        for c in range(3):
            def step(i, carry):
                for j in range(GROUP):
                    row = i * GROUP + j
                    mbuf[group, c, row] = (raw[c, row, pl.ds(first, 16), :] * scale).astype(BF16)
                return carry

            lax.fori_loop(0, HALF // GROUP, step, 0)

    def modes_copy(k):
        peer = z_peer(k)
        return remote(
            mbuf.at[peer], out.at[:, my_layer, pl.ds(my_low, HALF)],
            m_ss.at[k], m_rs.at[k], {"snap": peer},
        )

    for k in order:
        modes_for(z_peer(k))
        modes_copy(k).start()
    modes_for(z)
    own_modes = pltpu.make_async_copy(
        mbuf.at[z], out.at[:, my_layer, pl.ds(my_low, HALF)], m_ss.at[0]
    )
    own_modes.start()

    for k in range(1, nz):
        g_copy0(k).wait_recv()
    g_got0[z] = g_own[pl.ds(pl.multiple_of(z * 16, 16), 16), :]
    rows = g_got0[0]
    for i in range(1, nz):
        rows = rows + g_got0[i]
    for stage in (1, 2):
        count, mine, _ = stages[stage]
        g_send[stage] = rows
        g_got[stage, mine] = rows
        for k in range(1, count):
            g_copy(stage, k).start()
        for k in range(1, count):
            g_copy(stage, k).wait_recv()
        rows = g_got[stage, 0]
        for i in range(1, count):
            rows = rows + g_got[stage, i]
    gram_out[...] = rows

    own_modes.wait()
    for k in order:
        modes_copy(k).wait_recv()
    for c in (2, 1):
        for side in (0, 1):
            halo(c, side).wait_send()
    for k in order:
        for c in range(3):
            part_send(c, k).wait_send()
        modes_copy(k).wait_send()
        g_copy0(k).wait_send()
    for stage, (count, _, _) in enumerate(stages):
        for k in range(1, count):
            e_copy(stage, k).wait_send()
            if stage:
                g_copy(stage, k).wait_send()


def per_device(ny, nz, nxc, cells, velocity, metric, volume, coeffs):
    vel = jnp.transpose(velocity, (1, 2, 3, 0, 4))
    any_space = pl.BlockSpec(memory_space=pl.ANY)
    vmem = pl.BlockSpec(memory_space=pltpu.VMEM)
    top = max(nz, ny, nxc)
    dma = pltpu.SemaphoreType.DMA
    modes, rows = pl.pallas_call(
        functools.partial(kernel, ny, nz, nxc, cells),
        out_shape=(
            jax.ShapeDtypeStruct(vel.shape, BF16),
            jax.ShapeDtypeStruct((16, 128), F32),
        ),
        in_specs=[any_space, vmem, vmem, vmem],
        out_specs=(any_space, vmem),
        scratch_shapes=[
            pltpu.VMEM((3, 8, 36, 16, 128), BF16),
            pltpu.VMEM((3, 4, 32, 16, 128), BF16),
            pltpu.VMEM((3, HALF, nz, 16, 128), BF16),
            pltpu.VMEM((3, HALF, 128, 128), F32),
            pltpu.VMEM((nz, 3, HALF, 16, 128), BF16),
            pltpu.VMEM((128, 128), BF16),
            pltpu.VMEM((128, 128), F32),
            pltpu.VMEM((128, 128), F32),
            pltpu.VMEM((3, 8, 128), F32),
            pltpu.VMEM((3, top, 8, 128), F32),
            pltpu.VMEM((128, 128), F32),
            pltpu.VMEM((nz, 16, 128), F32),
            pltpu.VMEM((3, 16, 128), F32),
            pltpu.VMEM((3, top, 16, 128), F32),
            dma((3,)), dma((4,)), dma((4,)), dma((3, nz)), dma((3, nz)), dma((nz,)), dma((nz,)),
            dma((3, top)), dma((3, top)), dma((3, top)), dma((3, top)),
        ],
        compiler_params=pltpu.CompilerParams(
            collective_id=0, has_side_effects=True, vmem_limit_bytes=48 * 1024 * 1024
        ),
        name="pod",
    )(vel, metric, volume, coeffs)
    return rows, jnp.transpose(modes, (3, 0, 1, 2, 4))


def solution(mesh):
    nz = mesh.shape["snap"]
    nspace = mesh.shape["space"]
    ny = min(8, nspace // 2)
    placed = (
        P("snap", None, "space", None, None),
        P(None, "space", None, None),
        P("space", None, None),
        P(),
    )
    return jax.shard_map(
        functools.partial(per_device, ny, nz, nspace // ny, 3.0 * nspace * 4 * 32 * 128),
        mesh=mesh,
        in_specs=placed,
        out_specs=(P("snap", None), P("snap", None, "space", None, None)),
        check_vma=False,
    )
```

```python
import functools

import jax
import jax.numpy as jnp
from jax import lax
from jax.experimental import pallas as pl
from jax.experimental.pallas import tpu as pltpu
from jax.sharding import PartitionSpec as P

EPS = 1e-06
MESH = pl.DeviceIdType.MESH
F32 = jnp.float32
BF16 = jnp.bfloat16
HALF = 16
GROUP = 4
EARLY = 8


def remote(src, dst, send, recv, where):
    return pltpu.make_async_remote_copy(
        src_ref=src, dst_ref=dst, send_sem=send, recv_sem=recv,
        device_id=where, device_id_type=MESH,
    )


def kernel(
    ny, nz, nxc, cells,
    vel, metric_in, volume_in, coeffs_in,
    out, gram_out,
    stage, metric, volume, coeffs, ext, vort, got, raw, mbuf, early, land, coeff_t, acc, col,
    e_send, e_got, g_own, g_got0, g_send, g_got,
    local_sem, halo_ss, halo_rs, a_ss, a_rs, m_ss, m_rs, f_ss, f_rs, e_ss, e_rs, g_ss, g_rs,
):
    s = lax.axis_index("space")
    z = lax.axis_index("snap")
    nspace = ny * nxc
    core, iy, ix = lax.rem(s, 2), lax.rem(s // 2, ny), s // (2 * ny)
    q = ix * 2 + core
    left, right = lax.rem(s + nspace - 1, nspace), lax.rem(s + 1, nspace)

    def z_peer(k):
        return lax.rem(z + k, nz)

    def y_peer(k):
        return (ix * ny + lax.rem(iy + k, ny)) * 2 + core

    def q_peer(k):
        other = lax.rem(q + k, nxc)
        return ((other // 2) * ny + iy) * 2 + lax.rem(other, 2)

    barrier = pltpu.get_barrier_semaphore()
    for k in range(1, nz):
        pl.semaphore_signal(barrier, inc=1, device_id={"snap": z_peer(k)}, device_id_type=MESH)
    for k in range(1, ny):
        pl.semaphore_signal(barrier, inc=1, device_id={"space": y_peer(k)}, device_id_type=MESH)
    for k in range(1, nxc):
        pl.semaphore_signal(barrier, inc=1, device_id={"space": q_peer(k)}, device_id_type=MESH)
    for side in (left, right):
        pl.semaphore_signal(barrier, inc=1, device_id={"space": side}, device_id_type=MESH)

    loads = [pltpu.make_async_copy(vel.at[:, c], stage.at[c], local_sem.at[c]) for c in range(3)]
    tables = [
        pltpu.make_async_copy(a, b, local_sem.at[3 + i])
        for i, (a, b) in enumerate(((metric_in, metric), (coeffs_in, coeffs), (volume_in, volume)))
    ]
    for copy in (loads[2], loads[1], tables[0], loads[0], tables[1], tables[2]):
        copy.start()
    blank = jnp.zeros((4, 2, 16, 128), BF16)
    for c in (0, 2):
        ext[c, 2:6, 0:2] = blank
        ext[c, 2:6, 34:36] = blank
    acc[...] = jnp.zeros_like(acc)

    def load(c):
        loads[c].wait()
        for layer in range(4):
            ext[c, 2 + layer, 2:34] = jnp.swapaxes(stage[c, :, layer], 0, 1)

    load(2)
    load(1)
    tables[0].wait()

    def tile(c, layer, row):
        return ext[c, layer, row].astype(F32)

    def stencil(a, b, c, d):
        return 8.0 * (c - b) - (d - a)

    def along_x(c, layer, row):
        return stencil(*[tile(c, layer + o, row + 2) for o in (0, 1, 3, 4)])

    def along_y(c, layer, row):
        return stencil(*[tile(c, layer + 2, row + o) for o in (0, 1, 3, 4)])

    def along_z(c, layer, row):
        f = tile(c, layer + 2, row + 2)
        return stencil(*[pltpu.roll(f, o % 128, 1) for o in (2, 1, -1, -2)])

    def factor(d, layer, row):
        return metric[d, layer, pl.ds(row, 1), :] * (1.0 / 12.0)

    def curl(c, layer, row):
        if c == 0:
            a = along_y(2, layer, row) * factor(1, layer, row)
            b = along_z(1, layer, row) * factor(2, layer, row)
        elif c == 1:
            a = along_z(0, layer, row) * factor(2, layer, row)
            b = along_x(2, layer, row) * factor(0, layer, row)
        else:
            a = along_x(1, layer, row) * factor(0, layer, row)
            b = along_y(0, layer, row) * factor(1, layer, row)
        return (a - b).astype(BF16)

    def place(part):
        return part // 2, lax.rem(part, 2) * HALF

    def part_curl(c, part, own=False):
        layer, low = place(part)

        def step(i, carry):
            for j in range(GROUP):
                row = i * GROUP + j
                value = curl(c, layer, low + row)
                if own:
                    got[c, row, z] = value
                else:
                    vort[c, layer, low + row] = value
            return carry

        lax.fori_loop(0, HALF // GROUP, step, 0)

    def part_send(c, k):
        peer = z_peer(k)
        layer, low = place(peer)
        return remote(
            vort.at[c, layer, pl.ds(low, HALF)], got.at[c, :, z],
            a_ss.at[c, k], a_rs.at[c, k], {"snap": peer},
        )

    order = [k for pair in zip(range(nz // 2, 0, -1), range(nz // 2 + 1, nz + 1)) for k in pair]
    order = [k for k in order if k < nz]

    def exchange(c, ahead=0, enter=None):
        for n, k in enumerate(order):
            part_curl(c, z_peer(k))
            if enter is not None and n == ahead:
                enter()
                for earlier in order[:n]:
                    part_send(c, earlier).start()
            if enter is None or n >= ahead:
                part_send(c, k).start()
        part_curl(c, z, own=True)

    def halo(c, side):
        n = 2 * (2 - c) + side
        if side == 0:
            return remote(
                ext.at[c, 2:4, 2:34], ext.at[c, 6:8, 2:34], halo_ss.at[n], halo_rs.at[n], {"space": left}
            )
        return remote(
            ext.at[c, 4:6, 2:34], ext.at[c, 0:2, 2:34], halo_ss.at[n], halo_rs.at[n], {"space": right}
        )

    def enter():
        pl.semaphore_wait(barrier, (nz - 1) + (ny - 1) + (nxc - 1) + 2)
        for c in (2, 1):
            for side in (0, 1):
                halo(c, side).start()

    exchange(0, 2, enter)
    load(0)
    for copy in tables[1:]:
        copy.wait()
    coeff_t[...] = coeffs[...].astype(F32).T.astype(BF16)
    for c, needs in ((1, 2), (2, 1)):
        for side in (0, 1):
            halo(needs, side).wait_recv()
        exchange(c)

    my_layer, my_low = place(z)

    def wide(c, i):
        rows = [got[c, i * GROUP + j].reshape(128, 128) for j in range(GROUP)]
        return jnp.concatenate(rows, axis=1)

    def arrived(c):
        for k in order:
            part_send(c, k).wait_recv()

    def gram_of(c):
        def step(i, carry):
            v = wide(c, i)
            cells_volume = jnp.concatenate(
                [volume[my_layer, pl.ds(my_low + i * GROUP + j, 1), :] for j in range(GROUP)], axis=1
            )
            w = (v.astype(F32) * cells_volume).astype(BF16)
            acc[...] += lax.dot_general(w, v, (((1,), (1,)), ((), ())), preferred_element_type=F32)
            return carry

        lax.fori_loop(0, HALF // GROUP, step, 0)

    def raw_of(c):
        def step(i, carry):
            r = jnp.dot(coeff_t[...], wide(c, i), preferred_element_type=F32)
            for j in range(GROUP):
                raw[c, i * GROUP + j] = r[:, 128 * j : 128 * (j + 1)]
            return carry

        lax.fori_loop(0, HALF // GROUP, step, 0)

    for c in range(3):
        arrived(c)
        gram_of(c)
        if c < 2:
            raw_of(c)

    g_own[...] = acc[...] * (1.0 / cells)
    coeff_f = coeffs[...].astype(F32)
    product = jnp.dot(g_own[...], coeff_f, precision=lax.Precision.HIGHEST, preferred_element_type=F32)
    partial_e = jnp.sum((product * coeff_f).reshape(16, 8, 128), axis=0)
    stages = (
        (nz, z, lambda k: {"snap": z_peer(k)}),
        (ny, iy, lambda k: {"space": y_peer(k)}),
        (nxc, q, lambda k: {"space": q_peer(k)}),
    )

    def e_copy(stage, k):
        _, mine, where = stages[stage]
        return remote(
            e_send.at[stage], e_got.at[stage, mine], e_ss.at[stage, k], e_rs.at[stage, k], where(k)
        )

    def g_copy0(k):
        peer = z_peer(k)
        return remote(
            g_own.at[pl.ds(pl.multiple_of(peer * 16, 16), 16)], g_got0.at[z],
            g_ss.at[0, k], g_rs.at[0, k], {"snap": peer},
        )

    def g_copy(stage, k):
        _, mine, where = stages[stage]
        return remote(
            g_send.at[stage], g_got.at[stage, mine], g_ss.at[stage, k], g_rs.at[stage, k], where(k)
        )

    def early_copy(k):
        peer = z_peer(k)
        return remote(
            raw.at[0, 0:EARLY, pl.ds(pl.multiple_of(peer * 16, 16), 16)], early.at[z],
            f_ss.at[k], f_rs.at[k], {"snap": peer},
        )

    for step_of, (count, mine, _) in enumerate(stages):
        e_send[step_of] = partial_e
        e_got[step_of, mine] = partial_e
        for k in range(1, count):
            e_copy(step_of, k).start()
        if step_of == 0:
            for k in order:
                early_copy(k).start()
            for k in range(1, nz):
                g_copy0(k).start()
            raw_of(2)
        for k in range(1, count):
            e_copy(step_of, k).wait_recv()
        partial_e = e_got[step_of, 0]
        for i in range(1, count):
            partial_e = partial_e + e_got[step_of, i]
    energy = jnp.sum(partial_e, axis=0, keepdims=True)
    inverse = 1.0 / jnp.sqrt(energy + EPS)
    at_row = lax.broadcasted_iota(jnp.int32, (128, 128), 0)
    at_lane = lax.broadcasted_iota(jnp.int32, (128, 128), 1)
    diagonal = jnp.where(at_row == at_lane, jnp.broadcast_to(inverse, (128, 128)), 0.0)
    col[...] = jnp.broadcast_to(jnp.sum(diagonal, axis=1, keepdims=True), (128, 128))

    def modes_for(group, own=False):
        first = pl.multiple_of(group * 16, 16)
        scale = col[pl.ds(first, 16), :]

        def step(i, carry):
            for c in range(3):
                if c == 0 and not own:
                    rows = [EARLY + i * (HALF - EARLY) // 4 + j for j in range((HALF - EARLY) // 4)]
                else:
                    rows = [i * GROUP + j for j in range(GROUP)]
                for row in rows:
                    value = (raw[c, row, pl.ds(first, 16), :] * scale).astype(BF16)
                    if own:
                        land[c, my_layer, my_low + row] = value
                    else:
                        mbuf[group, c, row] = value
            return carry

        lax.fori_loop(0, HALF // GROUP, step, 0)

    def modes_copies(k):
        peer = z_peer(k)
        return (
            remote(
                mbuf.at[peer, 0, EARLY:HALF],
                land.at[0, my_layer, pl.ds(my_low + EARLY, HALF - EARLY)],
                m_ss.at[0, k], m_rs.at[0, k], {"snap": peer},
            ),
            remote(
                mbuf.at[peer, 1:3], land.at[1:3, my_layer, pl.ds(my_low, HALF)],
                m_ss.at[1, k], m_rs.at[1, k], {"snap": peer},
            ),
        )

    for k in order:
        modes_for(z_peer(k))
        for copy in modes_copies(k):
            copy.start()
    modes_for(z, own=True)

    my_scale = col[pl.ds(pl.multiple_of(z * 16, 16), 16), :]
    for k in order:
        early_copy(k).wait_recv()
        source = lax.rem(z + nz - k, nz)
        layer, low = place(source)
        for row in range(EARLY):
            land[0, layer, low + row] = (early[source, row] * my_scale).astype(BF16)

    for k in range(1, nz):
        g_copy0(k).wait_recv()
    g_got0[z] = g_own[pl.ds(pl.multiple_of(z * 16, 16), 16), :]
    rows = g_got0[0]
    for i in range(1, nz):
        rows = rows + g_got0[i]
    for step_of in (1, 2):
        count, mine, _ = stages[step_of]
        g_send[step_of] = rows
        g_got[step_of, mine] = rows
        for k in range(1, count):
            g_copy(step_of, k).start()
        for k in range(1, count):
            g_copy(step_of, k).wait_recv()
        rows = g_got[step_of, 0]
        for i in range(1, count):
            rows = rows + g_got[step_of, i]
    gram_out[...] = rows

    def deliver(source):
        layer, low = place(source)
        rows_at = pl.ds(pl.multiple_of(low, HALF), HALF)
        for c in range(3):
            out[:, c, layer, rows_at, :] = jnp.swapaxes(land[c, layer, rows_at], 0, 1)

    deliver(z)
    for k in order[::-1]:
        for copy in modes_copies(k):
            copy.wait_recv()
        deliver(lax.rem(z + nz - k, nz))
    for c in (2, 1):
        for side in (0, 1):
            halo(c, side).wait_send()
    for k in order:
        for c in range(3):
            part_send(c, k).wait_send()
        for copy in modes_copies(k):
            copy.wait_send()
        early_copy(k).wait_send()
        g_copy0(k).wait_send()
    for step_of, (count, _, _) in enumerate(stages):
        for k in range(1, count):
            e_copy(step_of, k).wait_send()
            if step_of:
                g_copy(step_of, k).wait_send()


def keep(modes, rows, modes_out, rows_out, sem):
    copies = [
        pltpu.make_async_copy(modes, modes_out, sem.at[0]),
        pltpu.make_async_copy(rows, rows_out, sem.at[1]),
    ]
    for copy in copies:
        copy.start()
    for copy in copies:
        copy.wait()


def per_device(ny, nz, nxc, cells, velocity, metric, volume, coeffs):
    any_space = pl.BlockSpec(memory_space=pl.ANY)
    vmem = pl.BlockSpec(memory_space=pltpu.VMEM)
    top = max(nz, ny, nxc)
    dma = pltpu.SemaphoreType.DMA
    modes, rows = pl.pallas_call(
        functools.partial(kernel, ny, nz, nxc, cells),
        out_shape=(
            jax.ShapeDtypeStruct(velocity.shape, BF16),
            jax.ShapeDtypeStruct((16, 128), F32),
        ),
        in_specs=[any_space] * 4,
        out_specs=(vmem, vmem),
        scratch_shapes=[
            pltpu.VMEM((3, 16, 4, 32, 128), BF16),
            pltpu.VMEM(metric.shape, F32),
            pltpu.VMEM(volume.shape, F32),
            pltpu.VMEM(coeffs.shape, BF16),
            pltpu.VMEM((3, 8, 36, 16, 128), BF16),
            pltpu.VMEM((3, 4, 32, 16, 128), BF16),
            pltpu.VMEM((3, HALF, nz, 16, 128), BF16),
            pltpu.VMEM((3, HALF, 128, 128), F32),
            pltpu.VMEM((nz, 3, HALF, 16, 128), BF16),
            pltpu.VMEM((nz, EARLY, 16, 128), F32),
            pltpu.VMEM((3, 4, 32, 16, 128), BF16),
            pltpu.VMEM((128, 128), BF16),
            pltpu.VMEM((128, 128), F32),
            pltpu.VMEM((128, 128), F32),
            pltpu.VMEM((3, 8, 128), F32),
            pltpu.VMEM((3, top, 8, 128), F32),
            pltpu.VMEM((128, 128), F32),
            pltpu.VMEM((nz, 16, 128), F32),
            pltpu.VMEM((3, 16, 128), F32),
            pltpu.VMEM((3, top, 16, 128), F32),
            dma((6,)), dma((4,)), dma((4,)), dma((3, nz)), dma((3, nz)), dma((2, nz)), dma((2, nz)),
            dma((nz,)), dma((nz,)),
            dma((3, top)), dma((3, top)), dma((3, top)), dma((3, top)),
        ],
        compiler_params=pltpu.CompilerParams(
            collective_id=0, has_side_effects=True, vmem_limit_bytes=48 * 1024 * 1024
        ),
        name="pod",
    )(*[pltpu.with_memory_space_constraint(a, pltpu.HBM) for a in (velocity, metric, volume, coeffs)])
    modes, rows = pl.pallas_call(
        keep,
        out_shape=(
            jax.ShapeDtypeStruct(modes.shape, BF16),
            jax.ShapeDtypeStruct(rows.shape, F32),
        ),
        in_specs=[any_space, any_space],
        out_specs=(any_space, any_space),
        scratch_shapes=[dma((2,))],
        compiler_params=pltpu.CompilerParams(vmem_limit_bytes=1024 * 1024),
        name="keep",
    )(modes, rows)
    return rows, modes


def solution(mesh):
    nz = mesh.shape["snap"]
    nspace = mesh.shape["space"]
    ny = min(8, nspace // 2)
    placed = (
        P("snap", None, "space", None, None),
        P(None, "space", None, None),
        P("space", None, None),
        P(),
    )
    return jax.shard_map(
        functools.partial(per_device, ny, nz, nspace // ny, 3.0 * nspace * 4 * 32 * 128),
        mesh=mesh,
        in_specs=placed,
        out_specs=(P("snap", None), P("snap", None, "space", None, None)),
        check_vma=False,
    )
```

```python
import functools

import jax
import jax.numpy as jnp
from jax import lax
from jax.experimental import pallas as pl
from jax.experimental.pallas import tpu as pltpu
from jax.sharding import PartitionSpec as P

EPS = 1e-06
MESH = pl.DeviceIdType.MESH
F32 = jnp.float32
BF16 = jnp.bfloat16
HALF = 16
GROUP = 4
PIECES = ((0, 0, 16), (1, 0, 16), (2, 0, 12), (2, 12, 4))
EARLY = 8


def remote(src, dst, send, recv, where):
    return pltpu.make_async_remote_copy(
        src_ref=src, dst_ref=dst, send_sem=send, recv_sem=recv,
        device_id=where, device_id_type=MESH,
    )


def kernel(
    ny, nz, nxc, cells,
    vel, metric_in, volume_in, coeffs_in,
    out, gram_out,
    stage, metric, volume, coeffs, ext, vort, got, raw, mbuf, early, land, coeff_t, acc, col,
    e_send, e_got, g_own, g_send, g_got,
    local_sem, halo_ss, halo_rs, a_ss, a_rs, m_ss, m_rs, f_ss, f_rs, e_ss, e_rs, g_ss, g_rs,
):
    s = lax.axis_index("space")
    z = lax.axis_index("snap")
    nspace = ny * nxc
    core, iy, ix = lax.rem(s, 2), lax.rem(s // 2, ny), s // (2 * ny)
    q = ix * 2 + core
    left, right = lax.rem(s + nspace - 1, nspace), lax.rem(s + 1, nspace)

    def z_peer(k):
        return lax.rem(z + k, nz)

    def y_peer(k):
        return (ix * ny + lax.rem(iy + k, ny)) * 2 + core

    def q_peer(k):
        other = lax.rem(q + k, nxc)
        return ((other // 2) * ny + iy) * 2 + lax.rem(other, 2)

    barrier = pltpu.get_barrier_semaphore()
    for k in range(1, nz):
        pl.semaphore_signal(barrier, inc=1, device_id={"snap": z_peer(k)}, device_id_type=MESH)
    for k in range(1, ny):
        pl.semaphore_signal(barrier, inc=1, device_id={"space": y_peer(k)}, device_id_type=MESH)
    for k in range(1, nxc):
        pl.semaphore_signal(barrier, inc=1, device_id={"space": q_peer(k)}, device_id_type=MESH)
    for side in (left, right):
        pl.semaphore_signal(barrier, inc=1, device_id={"space": side}, device_id_type=MESH)

    loads = [pltpu.make_async_copy(vel.at[:, c], stage.at[c], local_sem.at[c]) for c in range(3)]
    tables = [
        pltpu.make_async_copy(a, b, local_sem.at[3 + i])
        for i, (a, b) in enumerate(((metric_in, metric), (coeffs_in, coeffs), (volume_in, volume)))
    ]
    for copy in (loads[2], loads[1], tables[0], loads[0], tables[1], tables[2]):
        copy.start()
    blank = jnp.zeros((4, 2, 16, 128), BF16)
    for c in (0, 2):
        ext[c, 2:6, 0:2] = blank
        ext[c, 2:6, 34:36] = blank
    acc[...] = jnp.zeros_like(acc)

    def load(c):
        loads[c].wait()
        for layer in range(4):
            ext[c, 2 + layer, 2:34] = jnp.swapaxes(stage[c, :, layer], 0, 1)

    load(2)
    load(1)
    tables[0].wait()

    def tile(c, layer, row):
        return ext[c, layer, row].astype(F32)

    def stencil(a, b, c, d):
        return 8.0 * (c - b) - (d - a)

    def along_x(c, layer, row):
        return stencil(*[tile(c, layer + o, row + 2) for o in (0, 1, 3, 4)])

    def along_y(c, layer, row):
        return stencil(*[tile(c, layer + 2, row + o) for o in (0, 1, 3, 4)])

    def along_z(c, layer, row):
        f = tile(c, layer + 2, row + 2)
        return stencil(*[pltpu.roll(f, o % 128, 1) for o in (2, 1, -1, -2)])

    def factor(d, layer, row):
        return metric[d, layer, pl.ds(row, 1), :] * (1.0 / 12.0)

    def curl(c, layer, row):
        if c == 0:
            a = along_y(2, layer, row) * factor(1, layer, row)
            b = along_z(1, layer, row) * factor(2, layer, row)
        elif c == 1:
            a = along_z(0, layer, row) * factor(2, layer, row)
            b = along_x(2, layer, row) * factor(0, layer, row)
        else:
            a = along_x(1, layer, row) * factor(0, layer, row)
            b = along_y(0, layer, row) * factor(1, layer, row)
        return (a - b).astype(BF16)

    def place(part):
        return part // 2, lax.rem(part, 2) * HALF

    def part_curl(piece, part, own=False):
        c, first, count = piece
        layer, low = place(part)

        def step(i, carry):
            for j in range(GROUP):
                row = first + i * GROUP + j
                value = curl(c, layer, low + row)
                if own:
                    got[c, row, z] = value
                else:
                    vort[c, layer, low + row] = value
            return carry

        lax.fori_loop(0, count // GROUP, step, 0)

    def part_send(piece, k):
        c, first, count = piece
        n = PIECES.index(piece)
        peer = z_peer(k)
        layer, low = place(peer)
        return remote(
            vort.at[c, layer, pl.ds(low + first, count)], got.at[c, first : first + count, z],
            a_ss.at[n, k], a_rs.at[n, k], {"snap": peer},
        )

    order = [k for pair in zip(range(nz // 2, 0, -1), range(nz // 2 + 1, nz + 1)) for k in pair]
    order = [k for k in order if k < nz]

    def exchange(piece, ahead=0, enter=None):
        for n, k in enumerate(order):
            part_curl(piece, z_peer(k))
            if enter is not None and n == ahead:
                enter()
                for earlier in order[:n]:
                    part_send(piece, earlier).start()
            if enter is None or n >= ahead:
                part_send(piece, k).start()
        part_curl(piece, z, own=True)

    def halo(c, side):
        n = 2 * (2 - c) + side
        if side == 0:
            return remote(
                ext.at[c, 2:4, 2:34], ext.at[c, 6:8, 2:34], halo_ss.at[n], halo_rs.at[n], {"space": left}
            )
        return remote(
            ext.at[c, 4:6, 2:34], ext.at[c, 0:2, 2:34], halo_ss.at[n], halo_rs.at[n], {"space": right}
        )

    def enter():
        pl.semaphore_wait(barrier, (nz - 1) + (ny - 1) + (nxc - 1) + 2)
        for c in (2, 1):
            for side in (0, 1):
                halo(c, side).start()

    exchange(PIECES[0], 2, enter)
    load(0)
    for copy in tables[1:]:
        copy.wait()
    coeff_t[...] = coeffs[...].astype(F32).T.astype(BF16)
    for c, needs in ((1, 2), (2, 1)):
        for side in (0, 1):
            halo(needs, side).wait_recv()
        for piece in PIECES:
            if piece[0] == c:
                exchange(piece)

    my_layer, my_low = place(z)

    def wide(c, i):
        rows = [got[c, i * GROUP + j].reshape(128, 128) for j in range(GROUP)]
        return jnp.concatenate(rows, axis=1)

    def arrived(piece):
        for k in order:
            part_send(piece, k).wait_recv()

    def gram_of(piece):
        c, first, count = piece

        def step(i, carry):
            v = wide(c, i)
            cells_volume = jnp.concatenate(
                [volume[my_layer, pl.ds(my_low + i * GROUP + j, 1), :] for j in range(GROUP)], axis=1
            )
            w = (v.astype(F32) * cells_volume).astype(BF16)
            acc[...] += lax.dot_general(w, v, (((1,), (1,)), ((), ())), preferred_element_type=F32)
            return carry

        lax.fori_loop(first // GROUP, (first + count) // GROUP, step, 0)

    def raw_of(c):
        def step(i, carry):
            r = jnp.dot(coeff_t[...], wide(c, i), preferred_element_type=F32)
            for j in range(GROUP):
                raw[c, i * GROUP + j] = r[:, 128 * j : 128 * (j + 1)]
            return carry

        lax.fori_loop(0, HALF // GROUP, step, 0)

    for piece in PIECES:
        arrived(piece)
        gram_of(piece)
        if piece[0] < 2:
            raw_of(piece[0])

    g_own[...] = acc[...] * (1.0 / cells)
    coeff_f = coeffs[...].astype(F32)
    product = jnp.dot(g_own[...], coeff_f, precision=lax.Precision.HIGHEST, preferred_element_type=F32)
    partial_e = jnp.sum((product * coeff_f).reshape(16, 8, 128), axis=0)
    stages = (
        (nz, z, lambda k: {"snap": z_peer(k)}),
        (ny, iy, lambda k: {"space": y_peer(k)}),
        (nxc, q, lambda k: {"space": q_peer(k)}),
    )

    def e_copy(stage, k):
        _, mine, where = stages[stage]
        return remote(
            e_send.at[stage], e_got.at[stage, mine], e_ss.at[stage, k], e_rs.at[stage, k], where(k)
        )

    def g_rows(k):
        peer = lax.rem(iy + k, ny)
        return remote(
            g_own.at[pl.ds(pl.multiple_of(peer * 16, 16), 16)], g_got.at[0, iy],
            g_ss.at[0, k], g_rs.at[0, k], {"space": y_peer(k)},
        )

    def g_across(k):
        return remote(
            g_send.at[0], g_got.at[1, q], g_ss.at[1, k], g_rs.at[1, k], {"space": q_peer(k)}
        )

    def g_along(k):
        return remote(g_send.at[1], g_got.at[2, z], g_ss.at[2, k], g_rs.at[2, k], {"snap": z_peer(k)})

    def g_back(k):
        return remote(g_send.at[2], gram_out, g_ss.at[3, k], g_rs.at[3, k], {"space": y_peer(k)})

    def total(which, count):
        rows = g_got[which, 0]
        for i in range(1, count):
            rows = rows + g_got[which, i]
        return rows

    home = z == iy
    to_home = lax.rem(iy + nz - z, nz)

    def early_copy(k):
        peer = z_peer(k)
        return remote(
            raw.at[0, 0:EARLY, pl.ds(pl.multiple_of(peer * 16, 16), 16)], early.at[z],
            f_ss.at[k], f_rs.at[k], {"snap": peer},
        )

    for step_of, (count, mine, _) in enumerate(stages):
        e_send[step_of] = partial_e
        e_got[step_of, mine] = partial_e
        for k in order:
            e_copy(step_of, k).start()
        if step_of == 0:
            for k in range(1, ny):
                g_rows(k).start()
            raw_of(2)
        if step_of == 1:
            for k in order:
                early_copy(k).start()
            g_got[0, iy] = g_own[pl.ds(pl.multiple_of(iy * 16, 16), 16), :]
            for k in range(1, ny):
                g_rows(k).wait_recv()
            rows = total(0, ny)
            g_send[0] = rows
            g_got[1, q] = rows
            for k in range(1, nxc):
                g_across(k).start()
        if step_of == 2:
            for k in range(1, nxc):
                g_across(k).wait_recv()
            rows = total(1, nxc)
            g_send[1] = rows
            g_got[2, z] = rows

            @pl.when(jnp.logical_not(home))
            def _():
                g_along(to_home).start()

        for k in range(1, count):
            e_copy(step_of, k).wait_recv()
        partial_e = e_got[step_of, 0]
        for i in range(1, count):
            partial_e = partial_e + e_got[step_of, i]
    energy = jnp.sum(partial_e, axis=0, keepdims=True)
    inverse = 1.0 / jnp.sqrt(energy + EPS)
    at_row = lax.broadcasted_iota(jnp.int32, (128, 128), 0)
    at_lane = lax.broadcasted_iota(jnp.int32, (128, 128), 1)
    diagonal = jnp.where(at_row == at_lane, jnp.broadcast_to(inverse, (128, 128)), 0.0)
    col[...] = jnp.broadcast_to(jnp.sum(diagonal, axis=1, keepdims=True), (128, 128))

    def modes_for(group, own=False):
        first = pl.multiple_of(group * 16, 16)
        scale = col[pl.ds(first, 16), :]

        def put(c, row):
            value = (raw[c, row, pl.ds(first, 16), :] * scale).astype(BF16)
            if own:
                land[c, my_layer, my_low + row] = value
            else:
                mbuf[group, c, row] = value

        def step(i, carry):
            for c in (1, 2):
                for j in range(GROUP):
                    put(c, i * GROUP + j)
            return carry

        for row in range(0 if own else EARLY, HALF):
            put(0, row)
        lax.fori_loop(0, HALF // GROUP, step, 0)

    def modes_copies(k):
        peer = z_peer(k)
        return (
            remote(
                mbuf.at[peer, 0, EARLY:HALF],
                land.at[0, my_layer, pl.ds(my_low + EARLY, HALF - EARLY)],
                m_ss.at[0, k], m_rs.at[0, k], {"snap": peer},
            ),
            remote(
                mbuf.at[peer, 1:3], land.at[1:3, my_layer, pl.ds(my_low, HALF)],
                m_ss.at[1, k], m_rs.at[1, k], {"snap": peer},
            ),
        )

    for k in order:
        modes_for(z_peer(k))
        for copy in modes_copies(k):
            copy.start()
    modes_for(z, own=True)

    my_scale = col[pl.ds(pl.multiple_of(z * 16, 16), 16), :]
    for k in order:
        early_copy(k).wait_recv()
        source = lax.rem(z + nz - k, nz)
        layer, low = place(source)
        for row in range(EARLY):
            land[0, layer, low + row] = (early[source, row] * my_scale).astype(BF16)

    @pl.when(home)
    def _():
        for k in range(1, nz):
            g_along(k).wait_recv()
        rows = total(2, nz)
        g_send[2] = rows
        gram_out[...] = rows
        for k in range(1, ny):
            g_back(k).start()

    def deliver(source):
        layer, low = place(source)
        rows_at = pl.ds(pl.multiple_of(low, HALF), HALF)
        for c in range(3):
            out[:, c, layer, rows_at, :] = jnp.swapaxes(land[c, layer, rows_at], 0, 1)

    deliver(z)
    for k in order:
        for copy in modes_copies(k):
            copy.wait_recv()
        deliver(lax.rem(z + nz - k, nz))
    @pl.when(jnp.logical_not(home))
    def _():
        g_back(to_home).wait_recv()
        g_along(to_home).wait_send()

    @pl.when(home)
    def _():
        for k in range(1, ny):
            g_back(k).wait_send()

    for c in (2, 1):
        for side in (0, 1):
            halo(c, side).wait_send()
    for k in order:
        for piece in PIECES:
            part_send(piece, k).wait_send()
        for copy in modes_copies(k):
            copy.wait_send()
        early_copy(k).wait_send()
    for step_of, (count, _, _) in enumerate(stages):
        for k in range(1, count):
            e_copy(step_of, k).wait_send()
    for k in range(1, ny):
        g_rows(k).wait_send()
    for k in range(1, nxc):
        g_across(k).wait_send()


def keep(modes, rows, modes_out, rows_out, sem):
    copies = [pltpu.make_async_copy(rows, rows_out, sem.at[8])]
    for i in range(8):
        part = pl.ds(2 * i, 2)
        copies.append(pltpu.make_async_copy(modes.at[part], modes_out.at[part], sem.at[i]))
    for copy in copies:
        copy.start()
    for copy in copies:
        copy.wait()


def per_device(ny, nz, nxc, cells, velocity, metric, volume, coeffs):
    any_space = pl.BlockSpec(memory_space=pl.ANY)
    vmem = pl.BlockSpec(memory_space=pltpu.VMEM)
    top = max(nz, ny, nxc)
    dma = pltpu.SemaphoreType.DMA
    modes, rows = pl.pallas_call(
        functools.partial(kernel, ny, nz, nxc, cells),
        out_shape=(
            jax.ShapeDtypeStruct(velocity.shape, BF16),
            jax.ShapeDtypeStruct((16, 128), F32),
        ),
        in_specs=[any_space] * 4,
        out_specs=(vmem, vmem),
        scratch_shapes=[
            pltpu.VMEM((3, 16, 4, 32, 128), BF16),
            pltpu.VMEM(metric.shape, F32),
            pltpu.VMEM(volume.shape, F32),
            pltpu.VMEM(coeffs.shape, BF16),
            pltpu.VMEM((3, 8, 36, 16, 128), BF16),
            pltpu.VMEM((3, 4, 32, 16, 128), BF16),
            pltpu.VMEM((3, HALF, nz, 16, 128), BF16),
            pltpu.VMEM((3, HALF, 128, 128), F32),
            pltpu.VMEM((nz, 3, HALF, 16, 128), BF16),
            pltpu.VMEM((nz, EARLY, 16, 128), F32),
            pltpu.VMEM((3, 4, 32, 16, 128), BF16),
            pltpu.VMEM((128, 128), BF16),
            pltpu.VMEM((128, 128), F32),
            pltpu.VMEM((128, 128), F32),
            pltpu.VMEM((3, 8, 128), F32),
            pltpu.VMEM((3, top, 8, 128), F32),
            pltpu.VMEM((128, 128), F32),
            pltpu.VMEM((3, 16, 128), F32),
            pltpu.VMEM((3, top, 16, 128), F32),
            dma((6,)), dma((4,)), dma((4,)), dma((4, nz)), dma((4, nz)), dma((2, nz)), dma((2, nz)),
            dma((nz,)), dma((nz,)),
            dma((3, top)), dma((3, top)), dma((4, top)), dma((4, top)),
        ],
        compiler_params=pltpu.CompilerParams(
            collective_id=0, has_side_effects=True, vmem_limit_bytes=48 * 1024 * 1024
        ),
        name="pod",
    )(*[pltpu.with_memory_space_constraint(a, pltpu.HBM) for a in (velocity, metric, volume, coeffs)])
    modes, rows = pl.pallas_call(
        keep,
        out_shape=(
            jax.ShapeDtypeStruct(modes.shape, BF16),
            jax.ShapeDtypeStruct(rows.shape, F32),
        ),
        in_specs=[any_space, any_space],
        out_specs=(any_space, any_space),
        scratch_shapes=[dma((9,))],
        compiler_params=pltpu.CompilerParams(vmem_limit_bytes=1024 * 1024),
        name="keep",
    )(modes, rows)
    return rows, modes


def solution(mesh):
    nz = mesh.shape["snap"]
    nspace = mesh.shape["space"]
    ny = min(8, nspace // 2)
    placed = (
        P("snap", None, "space", None, None),
        P(None, "space", None, None),
        P("space", None, None),
        P(),
    )
    return jax.shard_map(
        functools.partial(per_device, ny, nz, nspace // ny, 3.0 * nspace * 4 * 32 * 128),
        mesh=mesh,
        in_specs=placed,
        out_specs=(P("snap", None), P("snap", None, "space", None, None)),
        check_vma=False,
    )
```

```python
import functools

import jax
import jax.numpy as jnp
from jax import lax
from jax.experimental import pallas as pl
from jax.experimental.pallas import tpu as pltpu
from jax.sharding import PartitionSpec as P

EPS = 1e-06
MESH = pl.DeviceIdType.MESH
F32 = jnp.float32
BF16 = jnp.bfloat16
HALF = 16
GROUP = 4
PIECES = ((0, 0, 16), (1, 0, 16), (2, 0, 12), (2, 12, 4))
EARLY_PARTS = ((0, 0, 3), (1, 3, 6))
EARLY = sum(rows for _, _, rows in EARLY_PARTS)


def remote(src, dst, send, recv, where):
    return pltpu.make_async_remote_copy(
        src_ref=src, dst_ref=dst, send_sem=send, recv_sem=recv,
        device_id=where, device_id_type=MESH,
    )


def kernel(
    ny, nz, nxc, cells,
    vel, metric_in, volume_in, coeffs_in,
    out, gram_out,
    stage, metric, volume, coeffs, ext, vort, got, raw, mbuf, early, land, coeff_t, acc, col,
    e_send, e_got, g_own, g_send, g_got,
    local_sem, halo_ss, halo_rs, a_ss, a_rs, m_ss, m_rs, f_ss, f_rs, e_ss, e_rs, g_ss, g_rs,
):
    s = lax.axis_index("space")
    z = lax.axis_index("snap")
    nspace = ny * nxc
    core, iy, ix = lax.rem(s, 2), lax.rem(s // 2, ny), s // (2 * ny)
    q = ix * 2 + core
    left, right = lax.rem(s + nspace - 1, nspace), lax.rem(s + 1, nspace)

    def z_peer(k):
        return lax.rem(z + k, nz)

    def y_peer(k):
        return (ix * ny + lax.rem(iy + k, ny)) * 2 + core

    def q_peer(k):
        other = lax.rem(q + k, nxc)
        return ((other // 2) * ny + iy) * 2 + lax.rem(other, 2)

    order = [k for pair in zip(range(nz // 2, 0, -1), range(nz // 2 + 1, nz + 1)) for k in pair]
    order = [k for k in order if k < nz]

    barrier = pltpu.get_barrier_semaphore()
    for k in order:
        pl.semaphore_signal(barrier, inc=1, device_id={"snap": z_peer(k)}, device_id_type=MESH)
    for k in range(1, ny):
        pl.semaphore_signal(barrier, inc=1, device_id={"space": y_peer(k)}, device_id_type=MESH)
    for k in range(1, nxc):
        pl.semaphore_signal(barrier, inc=1, device_id={"space": q_peer(k)}, device_id_type=MESH)
    for side in (left, right):
        pl.semaphore_signal(barrier, inc=1, device_id={"space": side}, device_id_type=MESH)

    loads = [pltpu.make_async_copy(vel.at[:, c], stage.at[c], local_sem.at[c]) for c in range(3)]
    tables = [
        pltpu.make_async_copy(a, b, local_sem.at[3 + i])
        for i, (a, b) in enumerate(((metric_in, metric), (coeffs_in, coeffs), (volume_in, volume)))
    ]
    for copy in (loads[2], loads[1], tables[0], loads[0], tables[1], tables[2]):
        copy.start()
    blank = jnp.zeros((4, 2, 16, 128), BF16)
    for c in (0, 2):
        ext[c, 2:6, 0:2] = blank
        ext[c, 2:6, 34:36] = blank
    acc[...] = jnp.zeros_like(acc)

    def load(c):
        loads[c].wait()
        for layer in range(4):
            ext[c, 2 + layer, 2:34] = jnp.swapaxes(stage[c, :, layer], 0, 1)

    load(2)
    load(1)
    tables[0].wait()

    def tile(c, layer, row):
        return ext[c, layer, row].astype(F32)

    def stencil(a, b, c, d):
        return 8.0 * (c - b) - (d - a)

    def along_x(c, layer, row):
        return stencil(*[tile(c, layer + o, row + 2) for o in (0, 1, 3, 4)])

    def along_y(c, layer, row):
        return stencil(*[tile(c, layer + 2, row + o) for o in (0, 1, 3, 4)])

    def along_z(c, layer, row):
        f = tile(c, layer + 2, row + 2)
        return stencil(*[pltpu.roll(f, o % 128, 1) for o in (2, 1, -1, -2)])

    def factor(d, layer, row):
        return metric[d, layer, pl.ds(row, 1), :] * (1.0 / 12.0)

    def curl(c, layer, row):
        if c == 0:
            a = along_y(2, layer, row) * factor(1, layer, row)
            b = along_z(1, layer, row) * factor(2, layer, row)
        elif c == 1:
            a = along_z(0, layer, row) * factor(2, layer, row)
            b = along_x(2, layer, row) * factor(0, layer, row)
        else:
            a = along_x(1, layer, row) * factor(0, layer, row)
            b = along_y(0, layer, row) * factor(1, layer, row)
        return (a - b).astype(BF16)

    def place(part):
        return part // 2, lax.rem(part, 2) * HALF

    def part_curl(piece, part, own=False):
        c, first, count = piece
        layer, low = place(part)

        def step(i, carry):
            for j in range(GROUP):
                row = first + i * GROUP + j
                value = curl(c, layer, low + row)
                if own:
                    got[c, row, z] = value
                else:
                    vort[c, layer, low + row] = value
            return carry

        lax.fori_loop(0, count // GROUP, step, 0)

    def part_send(piece, k):
        c, first, count = piece
        n = PIECES.index(piece)
        peer = z_peer(k)
        layer, low = place(peer)
        return remote(
            vort.at[c, layer, pl.ds(low + first, count)], got.at[c, first : first + count, z],
            a_ss.at[n, k], a_rs.at[n, k], {"snap": peer},
        )

    def exchange(piece, ahead=0, enter=None):
        for n, k in enumerate(order):
            part_curl(piece, z_peer(k))
            if enter is not None and n == ahead:
                enter()
                for earlier in order[:n]:
                    part_send(piece, earlier).start()
            if enter is None or n >= ahead:
                part_send(piece, k).start()
            if enter is not None and n == ahead:
                start_halo()
        part_curl(piece, z, own=True)

    def halo(c, side):
        n = 2 * (2 - c) + side
        if side == 0:
            return remote(
                ext.at[c, 2:4, 2:34], ext.at[c, 6:8, 2:34], halo_ss.at[n], halo_rs.at[n], {"space": left}
            )
        return remote(
            ext.at[c, 4:6, 2:34], ext.at[c, 0:2, 2:34], halo_ss.at[n], halo_rs.at[n], {"space": right}
        )

    def enter():
        pl.semaphore_wait(barrier, (nz - 1) + (ny - 1) + (nxc - 1) + 2)

    def start_halo():
        for c in (2, 1):
            for side in (0, 1):
                halo(c, side).start()

    exchange(PIECES[0], 2, enter)
    load(0)
    for copy in tables[1:]:
        copy.wait()
    coeff_t[...] = coeffs[...].astype(F32).T.astype(BF16)
    for c, needs in ((1, 2), (2, 1)):
        for side in (0, 1):
            halo(needs, side).wait_recv()
        for piece in PIECES:
            if piece[0] == c:
                exchange(piece)

    my_layer, my_low = place(z)

    def wide(c, i):
        rows = [got[c, i * GROUP + j].reshape(128, 128) for j in range(GROUP)]
        return jnp.concatenate(rows, axis=1)

    def arrived(piece):
        for k in order:
            part_send(piece, k).wait_recv()

    def gram_of(piece):
        c, first, count = piece

        def step(i, carry):
            v = wide(c, i)
            cells_volume = jnp.concatenate(
                [volume[my_layer, pl.ds(my_low + i * GROUP + j, 1), :] for j in range(GROUP)], axis=1
            )
            w = (v.astype(F32) * cells_volume).astype(BF16)
            acc[...] += lax.dot_general(w, v, (((1,), (1,)), ((), ())), preferred_element_type=F32)
            return carry

        lax.fori_loop(first // GROUP, (first + count) // GROUP, step, 0)

    def raw_of(c):
        def step(i, carry):
            r = jnp.dot(coeff_t[...], wide(c, i), preferred_element_type=F32)
            for j in range(GROUP):
                raw[c, i * GROUP + j] = r[:, 128 * j : 128 * (j + 1)]
            return carry

        lax.fori_loop(0, HALF // GROUP, step, 0)

    for piece in PIECES:
        arrived(piece)
        gram_of(piece)
        if piece[0] < 2:
            raw_of(piece[0])

    g_own[...] = acc[...] * (1.0 / cells)
    coeff_f = coeffs[...].astype(F32)
    product = jnp.dot(g_own[...], coeff_f, precision=lax.Precision.HIGHEST, preferred_element_type=F32)
    partial_e = jnp.sum((product * coeff_f).reshape(16, 8, 128), axis=0)
    stages = (
        (nz, z, lambda k: {"snap": z_peer(k)}),
        (ny, iy, lambda k: {"space": y_peer(k)}),
        (nxc, q, lambda k: {"space": q_peer(k)}),
    )

    def e_copy(stage, k):
        _, mine, where = stages[stage]
        return remote(
            e_send.at[stage], e_got.at[stage, mine], e_ss.at[stage, k], e_rs.at[stage, k], where(k)
        )

    def g_rows(k):
        peer = lax.rem(iy + k, ny)
        return remote(
            g_own.at[pl.ds(pl.multiple_of(peer * 16, 16), 16)], g_got.at[0, iy],
            g_ss.at[0, k], g_rs.at[0, k], {"space": y_peer(k)},
        )

    def g_across(k):
        return remote(
            g_send.at[0], g_got.at[1, q], g_ss.at[1, k], g_rs.at[1, k], {"space": q_peer(k)}
        )

    def g_along(k):
        return remote(g_send.at[1], g_got.at[2, z], g_ss.at[2, k], g_rs.at[2, k], {"snap": z_peer(k)})

    def g_back(k):
        return remote(g_send.at[2], gram_out, g_ss.at[3, k], g_rs.at[3, k], {"space": y_peer(k)})

    def total(which, count):
        rows = g_got[which, 0]
        for i in range(1, count):
            rows = rows + g_got[which, i]
        return rows

    home = z == iy
    to_home = lax.rem(iy + nz - z, nz)

    def early_copy(n, k):
        _, first, count = EARLY_PARTS[n]
        peer = z_peer(k)
        return remote(
            raw.at[0, first : first + count, pl.ds(pl.multiple_of(peer * 16, 16), 16)],
            early.at[z, first : first + count],
            f_ss.at[n, k], f_rs.at[n, k], {"snap": peer},
        )

    for step_of, (count, mine, _) in enumerate(stages):
        e_send[step_of] = partial_e
        e_got[step_of, mine] = partial_e
        for k in order:
            e_copy(step_of, k).start()
        for n, (when, _, _) in enumerate(EARLY_PARTS):
            if when == step_of:
                for k in order:
                    early_copy(n, k).start()
        if step_of == 0:
            for k in range(1, ny):
                g_rows(k).start()
            raw_of(2)
        if step_of == 1:
            g_got[0, iy] = g_own[pl.ds(pl.multiple_of(iy * 16, 16), 16), :]
            for k in range(1, ny):
                g_rows(k).wait_recv()
            rows = total(0, ny)
            g_send[0] = rows
            g_got[1, q] = rows
            for k in range(1, nxc):
                g_across(k).start()
        if step_of == 2:
            for k in range(1, nxc):
                g_across(k).wait_recv()
            rows = total(1, nxc)
            g_send[1] = rows
            g_got[2, z] = rows

            @pl.when(jnp.logical_not(home))
            def _():
                g_along(to_home).start()

        for k in range(1, count):
            e_copy(step_of, k).wait_recv()
        partial_e = e_got[step_of, 0]
        for i in range(1, count):
            partial_e = partial_e + e_got[step_of, i]
    energy = jnp.sum(partial_e, axis=0, keepdims=True)
    inverse = 1.0 / jnp.sqrt(energy + EPS)
    at_row = lax.broadcasted_iota(jnp.int32, (128, 128), 0)
    at_lane = lax.broadcasted_iota(jnp.int32, (128, 128), 1)
    diagonal = jnp.where(at_row == at_lane, jnp.broadcast_to(inverse, (128, 128)), 0.0)
    col[...] = jnp.broadcast_to(jnp.sum(diagonal, axis=1, keepdims=True), (128, 128))

    def modes_for(group, own=False):
        first = pl.multiple_of(group * 16, 16)
        scale = col[pl.ds(first, 16), :]

        def put(c, row):
            value = (raw[c, row, pl.ds(first, 16), :] * scale).astype(BF16)
            if own:
                land[c, my_layer, my_low + row] = value
            else:
                mbuf[group, c, row] = value

        def step(i, carry):
            for c in (1, 2):
                for j in range(GROUP):
                    put(c, i * GROUP + j)
            return carry

        for row in range(0 if own else EARLY, HALF):
            put(0, row)
        lax.fori_loop(0, HALF // GROUP, step, 0)

    def modes_copies(k):
        peer = z_peer(k)
        return (
            remote(
                mbuf.at[peer, 0, EARLY:HALF],
                land.at[0, my_layer, pl.ds(my_low + EARLY, HALF - EARLY)],
                m_ss.at[0, k], m_rs.at[0, k], {"snap": peer},
            ),
            remote(
                mbuf.at[peer, 1:3], land.at[1:3, my_layer, pl.ds(my_low, HALF)],
                m_ss.at[1, k], m_rs.at[1, k], {"snap": peer},
            ),
        )

    for k in order:
        modes_for(z_peer(k))
        for copy in modes_copies(k):
            copy.start()
    modes_for(z, own=True)

    my_scale = col[pl.ds(pl.multiple_of(z * 16, 16), 16), :]
    for k in order:
        for n in range(len(EARLY_PARTS)):
            early_copy(n, k).wait_recv()
        source = lax.rem(z + nz - k, nz)
        layer, low = place(source)
        for row in range(EARLY):
            land[0, layer, low + row] = (early[source, row] * my_scale).astype(BF16)

    for c in (2, 1):
        for side in (0, 1):
            halo(c, side).wait_send()
    for k in order:
        for piece in PIECES:
            part_send(piece, k).wait_send()
        for n in range(len(EARLY_PARTS)):
            early_copy(n, k).wait_send()
    for step_of, (count, _, _) in enumerate(stages):
        for k in range(1, count):
            e_copy(step_of, k).wait_send()
    for k in range(1, ny):
        g_rows(k).wait_send()
    for k in range(1, nxc):
        g_across(k).wait_send()

    @pl.when(home)
    def _():
        for k in range(1, nz):
            g_along(k).wait_recv()
        rows = total(2, nz)
        g_send[2] = rows
        gram_out[...] = rows
        for k in range(1, ny):
            g_back(k).start()

    def deliver(source):
        layer, low = place(source)
        rows_at = pl.ds(pl.multiple_of(low, HALF), HALF)
        for c in range(3):
            out[:, c, layer, rows_at, :] = jnp.swapaxes(land[c, layer, rows_at], 0, 1)

    deliver(z)
    for k in order:
        for copy in modes_copies(k):
            copy.wait_recv()
        deliver(lax.rem(z + nz - k, nz))
    for k in order:
        for copy in modes_copies(k):
            copy.wait_send()

    @pl.when(jnp.logical_not(home))
    def _():
        g_back(to_home).wait_recv()
        g_along(to_home).wait_send()

    @pl.when(home)
    def _():
        for k in range(1, ny):
            g_back(k).wait_send()


def keep(modes, rows, modes_out, rows_out, sem):
    copies = [pltpu.make_async_copy(rows, rows_out, sem.at[8])]
    for i in range(8):
        part = pl.ds(2 * i, 2)
        copies.append(pltpu.make_async_copy(modes.at[part], modes_out.at[part], sem.at[i]))
    for copy in copies:
        copy.start()
    for copy in copies:
        copy.wait()


def per_device(ny, nz, nxc, cells, velocity, metric, volume, coeffs):
    any_space = pl.BlockSpec(memory_space=pl.ANY)
    vmem = pl.BlockSpec(memory_space=pltpu.VMEM)
    top = max(nz, ny, nxc)
    dma = pltpu.SemaphoreType.DMA
    modes, rows = pl.pallas_call(
        functools.partial(kernel, ny, nz, nxc, cells),
        out_shape=(
            jax.ShapeDtypeStruct(velocity.shape, BF16),
            jax.ShapeDtypeStruct((16, 128), F32),
        ),
        in_specs=[any_space] * 4,
        out_specs=(vmem, vmem),
        scratch_shapes=[
            pltpu.VMEM((3, 16, 4, 32, 128), BF16),
            pltpu.VMEM(metric.shape, F32),
            pltpu.VMEM(volume.shape, F32),
            pltpu.VMEM(coeffs.shape, BF16),
            pltpu.VMEM((3, 8, 36, 16, 128), BF16),
            pltpu.VMEM((3, 4, 32, 16, 128), BF16),
            pltpu.VMEM((3, HALF, nz, 16, 128), BF16),
            pltpu.VMEM((3, HALF, 128, 128), F32),
            pltpu.VMEM((nz, 3, HALF, 16, 128), BF16),
            pltpu.VMEM((nz, EARLY, 16, 128), F32),
            pltpu.VMEM((3, 4, 32, 16, 128), BF16),
            pltpu.VMEM((128, 128), BF16),
            pltpu.VMEM((128, 128), F32),
            pltpu.VMEM((128, 128), F32),
            pltpu.VMEM((3, 8, 128), F32),
            pltpu.VMEM((3, top, 8, 128), F32),
            pltpu.VMEM((128, 128), F32),
            pltpu.VMEM((3, 16, 128), F32),
            pltpu.VMEM((3, top, 16, 128), F32),
            dma((6,)), dma((4,)), dma((4,)), dma((4, nz)), dma((4, nz)), dma((2, nz)), dma((2, nz)),
            dma((2, nz)), dma((2, nz)),
            dma((3, top)), dma((3, top)), dma((4, top)), dma((4, top)),
        ],
        compiler_params=pltpu.CompilerParams(
            collective_id=0, has_side_effects=True, vmem_limit_bytes=48 * 1024 * 1024
        ),
        name="pod",
    )(*[pltpu.with_memory_space_constraint(a, pltpu.HBM) for a in (velocity, metric, volume, coeffs)])
    modes, rows = pl.pallas_call(
        keep,
        out_shape=(
            jax.ShapeDtypeStruct(modes.shape, BF16),
            jax.ShapeDtypeStruct(rows.shape, F32),
        ),
        in_specs=[any_space, any_space],
        out_specs=(any_space, any_space),
        scratch_shapes=[dma((9,))],
        compiler_params=pltpu.CompilerParams(vmem_limit_bytes=1024 * 1024),
        name="keep",
    )(modes, rows)
    return rows, modes


def solution(mesh):
    nz = mesh.shape["snap"]
    nspace = mesh.shape["space"]
    ny = min(8, nspace // 2)
    placed = (
        P("snap", None, "space", None, None),
        P(None, "space", None, None),
        P("space", None, None),
        P(),
    )
    return jax.shard_map(
        functools.partial(per_device, ny, nz, nspace // ny, 3.0 * nspace * 4 * 32 * 128),
        mesh=mesh,
        in_specs=placed,
        out_specs=(P("snap", None), P("snap", None, "space", None, None)),
        check_vma=False,
    )
```

```python
import functools

import jax
import jax.numpy as jnp
from jax import lax
from jax.experimental import pallas as pl
from jax.experimental.pallas import tpu as pltpu
from jax.sharding import PartitionSpec as P

EPS = 1e-06
MESH = pl.DeviceIdType.MESH
F32 = jnp.float32
BF16 = jnp.bfloat16
HALF = 16
GROUP = 4
PIECES = ((0, 0, 16), (1, 0, 16), (2, 0, 12), (2, 12, 4))
EARLY_PARTS = ((0, 0, 4), (1, 4, 6))
EARLY = sum(rows for _, _, rows in EARLY_PARTS)


def remote(src, dst, send, recv, where):
    return pltpu.make_async_remote_copy(
        src_ref=src, dst_ref=dst, send_sem=send, recv_sem=recv,
        device_id=where, device_id_type=MESH,
    )


def kernel(
    ny, nz, nxc, cells,
    vel, metric_in, volume_in, coeffs_in,
    out, gram_out,
    stage, metric, volume, coeffs, ext, vort, got, raw, mbuf, early, land, coeff_t, acc, col,
    e_send, e_got, g_own, g_send, g_got,
    local_sem, halo_ss, halo_rs, a_ss, a_rs, m_ss, m_rs, f_ss, f_rs, e_ss, e_rs, g_ss, g_rs,
):
    s = lax.axis_index("space")
    z = lax.axis_index("snap")
    nspace = ny * nxc
    core, iy, ix = lax.rem(s, 2), lax.rem(s // 2, ny), s // (2 * ny)
    q = ix * 2 + core
    left, right = lax.rem(s + nspace - 1, nspace), lax.rem(s + 1, nspace)

    def z_peer(k):
        return lax.rem(z + k, nz)

    def y_peer(k):
        return (ix * ny + lax.rem(iy + k, ny)) * 2 + core

    def q_peer(k):
        other = lax.rem(q + k, nxc)
        return ((other // 2) * ny + iy) * 2 + lax.rem(other, 2)

    order = [k for pair in zip(range(nz // 2, 0, -1), range(nz // 2 + 1, nz + 1)) for k in pair]
    order = [k for k in order if k < nz]

    barrier = pltpu.get_barrier_semaphore()
    for k in order:
        pl.semaphore_signal(barrier, inc=1, device_id={"snap": z_peer(k)}, device_id_type=MESH)
    for k in range(1, ny):
        pl.semaphore_signal(barrier, inc=1, device_id={"space": y_peer(k)}, device_id_type=MESH)
    for k in range(1, nxc):
        pl.semaphore_signal(barrier, inc=1, device_id={"space": q_peer(k)}, device_id_type=MESH)
    for side in (left, right):
        pl.semaphore_signal(barrier, inc=1, device_id={"space": side}, device_id_type=MESH)

    loads = [pltpu.make_async_copy(vel.at[:, c], stage.at[c], local_sem.at[c]) for c in range(3)]
    tables = [
        pltpu.make_async_copy(a, b, local_sem.at[3 + i])
        for i, (a, b) in enumerate(((metric_in, metric), (coeffs_in, coeffs), (volume_in, volume)))
    ]
    for copy in (loads[2], loads[1], tables[0], loads[0], tables[1], tables[2]):
        copy.start()
    blank = jnp.zeros((4, 2, 16, 128), BF16)
    for c in (0, 2):
        ext[c, 2:6, 0:2] = blank
        ext[c, 2:6, 34:36] = blank
    acc[...] = jnp.zeros_like(acc)

    def load(c):
        loads[c].wait()
        for layer in range(4):
            ext[c, 2 + layer, 2:34] = jnp.swapaxes(stage[c, :, layer], 0, 1)

    load(2)
    load(1)
    tables[0].wait()

    def tile(c, layer, row):
        return ext[c, layer, row].astype(F32)

    def stencil(a, b, c, d):
        return 8.0 * (c - b) - (d - a)

    def along_x(c, layer, row):
        return stencil(*[tile(c, layer + o, row + 2) for o in (0, 1, 3, 4)])

    def along_y(c, layer, row):
        return stencil(*[tile(c, layer + 2, row + o) for o in (0, 1, 3, 4)])

    def along_z(c, layer, row):
        f = tile(c, layer + 2, row + 2)
        return stencil(*[pltpu.roll(f, o % 128, 1) for o in (2, 1, -1, -2)])

    def factor(d, layer, row):
        return metric[d, layer, pl.ds(row, 1), :] * (1.0 / 12.0)

    def curl(c, layer, row):
        if c == 0:
            a = along_y(2, layer, row) * factor(1, layer, row)
            b = along_z(1, layer, row) * factor(2, layer, row)
        elif c == 1:
            a = along_z(0, layer, row) * factor(2, layer, row)
            b = along_x(2, layer, row) * factor(0, layer, row)
        else:
            a = along_x(1, layer, row) * factor(0, layer, row)
            b = along_y(0, layer, row) * factor(1, layer, row)
        return (a - b).astype(BF16)

    def place(part):
        return part // 2, lax.rem(part, 2) * HALF

    def part_curl(piece, part, own=False):
        c, first, count = piece
        layer, low = place(part)

        def step(i, carry):
            for j in range(GROUP):
                row = first + i * GROUP + j
                value = curl(c, layer, low + row)
                if own:
                    got[c, row, z] = value
                else:
                    vort[c, layer, low + row] = value
            return carry

        lax.fori_loop(0, count // GROUP, step, 0)

    def part_send(piece, k):
        c, first, count = piece
        n = PIECES.index(piece)
        peer = z_peer(k)
        layer, low = place(peer)
        return remote(
            vort.at[c, layer, pl.ds(low + first, count)], got.at[c, first : first + count, z],
            a_ss.at[n, k], a_rs.at[n, k], {"snap": peer},
        )

    def exchange(piece, ahead=0, enter=None):
        for n, k in enumerate(order):
            part_curl(piece, z_peer(k))
            if enter is not None and n == ahead:
                enter()
                for earlier in order[:n]:
                    part_send(piece, earlier).start()
            if enter is None or n >= ahead:
                part_send(piece, k).start()
            if enter is not None and n == ahead:
                start_halo()
        part_curl(piece, z, own=True)

    def halo(c, side):
        n = 2 * (2 - c) + side
        if side == 0:
            return remote(
                ext.at[c, 2:4, 2:34], ext.at[c, 6:8, 2:34], halo_ss.at[n], halo_rs.at[n], {"space": left}
            )
        return remote(
            ext.at[c, 4:6, 2:34], ext.at[c, 0:2, 2:34], halo_ss.at[n], halo_rs.at[n], {"space": right}
        )

    def enter():
        pl.semaphore_wait(barrier, (nz - 1) + (ny - 1) + (nxc - 1) + 2)

    def start_halo():
        for c in (2, 1):
            for side in (0, 1):
                halo(c, side).start()

    exchange(PIECES[0], 2, enter)
    load(0)
    for copy in tables[1:]:
        copy.wait()
    coeff_t[...] = coeffs[...].astype(F32).T.astype(BF16)
    for c, needs in ((1, 2), (2, 1)):
        for side in (0, 1):
            halo(needs, side).wait_recv()
        for piece in PIECES:
            if piece[0] == c:
                exchange(piece)

    my_layer, my_low = place(z)

    def wide(c, i):
        rows = [got[c, i * GROUP + j].reshape(128, 128) for j in range(GROUP)]
        return jnp.concatenate(rows, axis=1)

    def arrived(piece):
        for k in order:
            part_send(piece, k).wait_recv()

    def gram_of(piece):
        c, first, count = piece

        def step(i, carry):
            v = wide(c, i)
            cells_volume = jnp.concatenate(
                [volume[my_layer, pl.ds(my_low + i * GROUP + j, 1), :] for j in range(GROUP)], axis=1
            )
            w = (v.astype(F32) * cells_volume).astype(BF16)
            acc[...] += lax.dot_general(w, v, (((1,), (1,)), ((), ())), preferred_element_type=F32)
            return carry

        lax.fori_loop(first // GROUP, (first + count) // GROUP, step, 0)

    def raw_of(c):
        def step(i, carry):
            r = jnp.dot(coeff_t[...], wide(c, i), preferred_element_type=F32)
            for j in range(GROUP):
                raw[c, i * GROUP + j] = r[:, 128 * j : 128 * (j + 1)]
            return carry

        lax.fori_loop(0, HALF // GROUP, step, 0)

    for piece in PIECES:
        arrived(piece)
        gram_of(piece)
        if piece[0] < 2:
            raw_of(piece[0])

    g_own[...] = acc[...] * (1.0 / cells)
    coeff_f = coeffs[...].astype(F32)
    product = jnp.dot(g_own[...], coeff_f, precision=lax.Precision.HIGHEST, preferred_element_type=F32)
    partial_e = jnp.sum((product * coeff_f).reshape(16, 8, 128), axis=0)
    stages = (
        (nz, z, lambda k: {"snap": z_peer(k)}),
        (ny, iy, lambda k: {"space": y_peer(k)}),
        (nxc, q, lambda k: {"space": q_peer(k)}),
    )

    def e_copy(stage, k):
        _, mine, where = stages[stage]
        return remote(
            e_send.at[stage], e_got.at[stage, mine], e_ss.at[stage, k], e_rs.at[stage, k], where(k)
        )

    def g_rows(k):
        peer = lax.rem(iy + k, ny)
        return remote(
            g_own.at[pl.ds(pl.multiple_of(peer * 16, 16), 16)], g_got.at[0, iy],
            g_ss.at[0, k], g_rs.at[0, k], {"space": y_peer(k)},
        )

    def g_across(k):
        return remote(
            g_send.at[0], g_got.at[1, q], g_ss.at[1, k], g_rs.at[1, k], {"space": q_peer(k)}
        )

    def g_along(k):
        return remote(g_send.at[1], g_got.at[2, z], g_ss.at[2, k], g_rs.at[2, k], {"snap": z_peer(k)})

    def g_back(k):
        return remote(g_send.at[2], gram_out, g_ss.at[3, k], g_rs.at[3, k], {"space": y_peer(k)})

    def total(which, count):
        rows = g_got[which, 0]
        for i in range(1, count):
            rows = rows + g_got[which, i]
        return rows

    home = z == iy
    to_home = lax.rem(iy + nz - z, nz)

    def early_copy(n, k):
        _, first, count = EARLY_PARTS[n]
        peer = z_peer(k)
        return remote(
            raw.at[0, first : first + count, pl.ds(pl.multiple_of(peer * 16, 16), 16)],
            early.at[z, first : first + count],
            f_ss.at[n, k], f_rs.at[n, k], {"snap": peer},
        )

    for step_of, (count, mine, _) in enumerate(stages):
        e_send[step_of] = partial_e
        e_got[step_of, mine] = partial_e
        for k in order:
            e_copy(step_of, k).start()
        for n, (when, _, _) in enumerate(EARLY_PARTS):
            if when == step_of:
                for k in order:
                    early_copy(n, k).start()
        if step_of == 0:
            for k in range(1, ny):
                g_rows(k).start()
            raw_of(2)
        if step_of == 1:
            g_got[0, iy] = g_own[pl.ds(pl.multiple_of(iy * 16, 16), 16), :]
            for k in range(1, ny):
                g_rows(k).wait_recv()
            rows = total(0, ny)
            g_send[0] = rows
            g_got[1, q] = rows
            for k in range(1, nxc):
                g_across(k).start()
        if step_of == 2:
            for k in range(1, nxc):
                g_across(k).wait_recv()
            rows = total(1, nxc)
            g_send[1] = rows
            g_got[2, z] = rows

            @pl.when(jnp.logical_not(home))
            def _():
                g_along(to_home).start()

        for k in range(1, count):
            e_copy(step_of, k).wait_recv()
        partial_e = e_got[step_of, 0]
        for i in range(1, count):
            partial_e = partial_e + e_got[step_of, i]
    energy = jnp.sum(partial_e, axis=0, keepdims=True)
    inverse = 1.0 / jnp.sqrt(energy + EPS)
    at_row = lax.broadcasted_iota(jnp.int32, (128, 128), 0)
    at_lane = lax.broadcasted_iota(jnp.int32, (128, 128), 1)
    diagonal = jnp.where(at_row == at_lane, jnp.broadcast_to(inverse, (128, 128)), 0.0)
    col[...] = jnp.broadcast_to(jnp.sum(diagonal, axis=1, keepdims=True), (128, 128))

    def modes_for(group, own=False):
        first = pl.multiple_of(group * 16, 16)
        scale = col[pl.ds(first, 16), :]

        def put(c, row):
            value = (raw[c, row, pl.ds(first, 16), :] * scale).astype(BF16)
            if own:
                land[c, my_layer, my_low + row] = value
            else:
                mbuf[group, c, row] = value

        def step(i, carry):
            for c in (1, 2):
                for j in range(GROUP):
                    put(c, i * GROUP + j)
            return carry

        for row in range(0 if own else EARLY, HALF):
            put(0, row)
        lax.fori_loop(0, HALF // GROUP, step, 0)

    def modes_copies(k):
        peer = z_peer(k)
        return (
            remote(
                mbuf.at[peer, 0, EARLY:HALF],
                land.at[0, my_layer, pl.ds(my_low + EARLY, HALF - EARLY)],
                m_ss.at[0, k], m_rs.at[0, k], {"snap": peer},
            ),
            remote(
                mbuf.at[peer, 1:3], land.at[1:3, my_layer, pl.ds(my_low, HALF)],
                m_ss.at[1, k], m_rs.at[1, k], {"snap": peer},
            ),
        )

    for k in order:
        modes_for(z_peer(k))
        for copy in modes_copies(k):
            copy.start()
    modes_for(z, own=True)

    my_scale = col[pl.ds(pl.multiple_of(z * 16, 16), 16), :]
    for k in order:
        for n in range(len(EARLY_PARTS)):
            early_copy(n, k).wait_recv()
        source = lax.rem(z + nz - k, nz)
        layer, low = place(source)
        for row in range(EARLY):
            land[0, layer, low + row] = (early[source, row] * my_scale).astype(BF16)

    for c in (2, 1):
        for side in (0, 1):
            halo(c, side).wait_send()
    for k in order:
        for piece in PIECES:
            part_send(piece, k).wait_send()
        for n in range(len(EARLY_PARTS)):
            early_copy(n, k).wait_send()
    for step_of, (count, _, _) in enumerate(stages):
        for k in range(1, count):
            e_copy(step_of, k).wait_send()
    for k in range(1, ny):
        g_rows(k).wait_send()
    for k in range(1, nxc):
        g_across(k).wait_send()

    @pl.when(home)
    def _():
        for k in range(1, nz):
            g_along(k).wait_recv()
        rows = total(2, nz)
        g_send[2] = rows
        gram_out[...] = rows
        for k in range(1, ny):
            g_back(k).start()

    def deliver(source):
        layer, low = place(source)
        rows_at = pl.ds(pl.multiple_of(low, HALF), HALF)
        for c in range(3):
            out[:, c, layer, rows_at, :] = jnp.swapaxes(land[c, layer, rows_at], 0, 1)

    deliver(z)
    for k in order:
        for copy in modes_copies(k):
            copy.wait_recv()
        deliver(lax.rem(z + nz - k, nz))
    for k in order:
        for copy in modes_copies(k):
            copy.wait_send()

    @pl.when(jnp.logical_not(home))
    def _():
        g_back(to_home).wait_recv()
        g_along(to_home).wait_send()

    @pl.when(home)
    def _():
        for k in range(1, ny):
            g_back(k).wait_send()


def keep(modes, rows, modes_out, rows_out, sem):
    copies = [pltpu.make_async_copy(rows, rows_out, sem.at[8])]
    for i in range(8):
        part = pl.ds(2 * i, 2)
        copies.append(pltpu.make_async_copy(modes.at[part], modes_out.at[part], sem.at[i]))
    for copy in copies:
        copy.start()
    for copy in copies:
        copy.wait()


def per_device(ny, nz, nxc, cells, velocity, metric, volume, coeffs):
    any_space = pl.BlockSpec(memory_space=pl.ANY)
    vmem = pl.BlockSpec(memory_space=pltpu.VMEM)
    top = max(nz, ny, nxc)
    dma = pltpu.SemaphoreType.DMA
    modes, rows = pl.pallas_call(
        functools.partial(kernel, ny, nz, nxc, cells),
        out_shape=(
            jax.ShapeDtypeStruct(velocity.shape, BF16),
            jax.ShapeDtypeStruct((16, 128), F32),
        ),
        in_specs=[any_space] * 4,
        out_specs=(vmem, vmem),
        scratch_shapes=[
            pltpu.VMEM((3, 16, 4, 32, 128), BF16),
            pltpu.VMEM(metric.shape, F32),
            pltpu.VMEM(volume.shape, F32),
            pltpu.VMEM(coeffs.shape, BF16),
            pltpu.VMEM((3, 8, 36, 16, 128), BF16),
            pltpu.VMEM((3, 4, 32, 16, 128), BF16),
            pltpu.VMEM((3, HALF, nz, 16, 128), BF16),
            pltpu.VMEM((3, HALF, 128, 128), F32),
            pltpu.VMEM((nz, 3, HALF, 16, 128), BF16),
            pltpu.VMEM((nz, EARLY, 16, 128), F32),
            pltpu.VMEM((3, 4, 32, 16, 128), BF16),
            pltpu.VMEM((128, 128), BF16),
            pltpu.VMEM((128, 128), F32),
            pltpu.VMEM((128, 128), F32),
            pltpu.VMEM((3, 8, 128), F32),
            pltpu.VMEM((3, top, 8, 128), F32),
            pltpu.VMEM((128, 128), F32),
            pltpu.VMEM((3, 16, 128), F32),
            pltpu.VMEM((3, top, 16, 128), F32),
            dma((6,)), dma((4,)), dma((4,)), dma((4, nz)), dma((4, nz)), dma((2, nz)), dma((2, nz)),
            dma((2, nz)), dma((2, nz)),
            dma((3, top)), dma((3, top)), dma((4, top)), dma((4, top)),
        ],
        compiler_params=pltpu.CompilerParams(
            collective_id=0, has_side_effects=True, vmem_limit_bytes=48 * 1024 * 1024
        ),
        name="pod",
    )(*[pltpu.with_memory_space_constraint(a, pltpu.HBM) for a in (velocity, metric, volume, coeffs)])
    modes, rows = pl.pallas_call(
        keep,
        out_shape=(
            jax.ShapeDtypeStruct(modes.shape, BF16),
            jax.ShapeDtypeStruct(rows.shape, F32),
        ),
        in_specs=[any_space, any_space],
        out_specs=(any_space, any_space),
        scratch_shapes=[dma((9,))],
        compiler_params=pltpu.CompilerParams(vmem_limit_bytes=1024 * 1024),
        name="keep",
    )(modes, rows)
    return rows, modes


def solution(mesh):
    nz = mesh.shape["snap"]
    nspace = mesh.shape["space"]
    ny = min(8, nspace // 2)
    placed = (
        P("snap", None, "space", None, None),
        P(None, "space", None, None),
        P("space", None, None),
        P(),
    )
    return jax.shard_map(
        functools.partial(per_device, ny, nz, nspace // ny, 3.0 * nspace * 4 * 32 * 128),
        mesh=mesh,
        in_specs=placed,
        out_specs=(P("snap", None), P("snap", None, "space", None, None)),
        check_vma=False,
    )
```
